32 devices in a mesh: dp: 8 (over y, x, core), tensor: 4 (over z).
Axes of the slice: x: 2, y: 2, z: 4, core: 2. Of those that a mesh axis runs over, the one named last changes fastest.
Arguments:
- inputs: bfloat16 [16384, 2048], P(('dp', 'tensor')), may hold values from -51 to 51
- w_query: bfloat16 [2048, 2048], P('dp', 'tensor'), may hold values from -1 to 1
- w_key: bfloat16 [2048, 2048], P('dp', 'tensor'), may hold values from -1 to 1
- w_value: bfloat16 [2048, 2048], P('dp', 'tensor'), may hold values from -0.125 to 0.125
- w_out: bfloat16 [2048, 2048], P('tensor', 'dp'), may hold values from -1.5 to 1.5
- gain_one: bfloat16 [2048], P('dp'), may hold values from 0.5 to 1.5
- w_gate: bfloat16 [2048, 8192], P('dp', 'tensor'), may hold values from -0.125 to 0.125
- w_up: bfloat16 [2048, 8192], P('dp', 'tensor'), may hold values from -0.125 to 0.125
- w_down: bfloat16 [8192, 2048], P('tensor', 'dp'), may hold values from -0.0625 to 0.0625
- gain_two: bfloat16 [2048], P('dp'), may hold values from 0.5 to 1.5
- cotangent: bfloat16 [16384, 2048], P(('dp', 'tensor')), may hold values from -6 to 6
Outputs:
- output: bfloat16 [16384, 2048], P(('dp', 'tensor'))
- input_grad: float32 [16384, 2048], P(('dp', 'tensor'))
- grad_query: float32 [2048, 2048], P('dp', 'tensor')
- grad_key: float32 [2048, 2048], P('dp', 'tensor')
- grad_value: float32 [2048, 2048], P('dp', 'tensor')
- grad_out: float32 [2048, 2048], P('tensor', 'dp')
- grad_gain_one: float32 [2048], P(('dp', 'tensor'))
- grad_gate: float32 [2048, 8192], P('dp', 'tensor')
- grad_up: float32 [2048, 8192], P('dp', 'tensor')
- grad_down: float32 [8192, 2048], P('tensor', 'dp')
- grad_gain_two: float32 [2048], P(('dp', 'tensor'))
The draws below stay inside these ranges and needn't reach their ends.
All inputs are finite; a program needn't handle non-finite values.
Results may differ from the reference program's by a relative error of at most 0.018.
Values may be sent and summed in bfloat16 or wider, within the bound.
No kernel may reach another device: no remote copies, remote signals or barrier semaphores. Data moves between devices by JAX's collectives and lax.ppermute only.
A program may use at most 184 MiB of HBM per device.

```python
import math
import jax
import jax.numpy as jnp
from jax import lax

D = 2048
H = 32
HD = 64
FF = 8192
SEQ_DP = 2
LEN = 1024
TOKENS = 16384
N_DP = 8


def draw_inputs(key, part):
    noise_part = jnp.clip(jax.random.normal(jax.random.fold_in(key, 1), (TOKENS, D), jnp.float32), -4.0, 4.0)
    row_scale = jnp.exp(jax.random.uniform(jax.random.fold_in(key, 2), (TOKENS, 1), jnp.float32, math.log(0.3), math.log(3.0)))
    col_scale = jnp.exp(jax.random.uniform(jax.random.fold_in(key, 3), (1, D), jnp.float32, math.log(0.3), math.log(3.0)))
    return (noise_part * row_scale * col_scale).astype(jnp.bfloat16)


def projection_draw(key, salt):
    return jnp.clip(jax.random.normal(jax.random.fold_in(key, salt), (D, D), jnp.float32), -4.0, 4.0) * D ** (-0.5)


def draw_w_query(key, part):
    return projection_draw(key, 21).astype(jnp.bfloat16)


def draw_w_key(key, part):
    return projection_draw(key, 22).astype(jnp.bfloat16)


def spiked(values, key, source, target, parts, factor):
    owner, partner = [(jnp.arange(values.shape[position]) // (values.shape[position] // parts)).reshape([-1 if axis == position else 1 for axis in range(values.ndim)]) for position in (source, target)]
    chosen = jax.random.permutation(key, parts)[partner]
    strong = (owner == chosen) | (owner == (partner + parts // 2) % parts)
    return jnp.where(strong, factor * values, values)


def levels(own_key, extent, pieces, low, top_value):
    def one(position, shards_of):
        heights = jax.random.uniform(jax.random.fold_in(jax.random.fold_in(own_key, 6), position), (shards_of,), jnp.float32, low / len(pieces), top_value / len(pieces))
        return jnp.repeat(jnp.exp(heights), extent[position] // shards_of).reshape((-1,) + (1,) * (len(extent) - position - 1))

    level = one(*pieces[0])
    for cut in pieces[1:]:
        level = level * one(*cut)
    return level


def scatter_about(key, dims, scale, most, split=(), held_as=jnp.bfloat16):
    values = jax.random.normal(key, dims, jnp.float32) * scale
    if len(split) > 0:
        values = levels(key, dims, split, -0.22, 0.18) * values
    return jnp.clip(values, min=-most, max=most).astype(held_as)


def heavy_noise(rng, shape, scale, limit, shards, heavy, kind=jnp.bfloat16):
    values = scale * jax.random.normal(rng, shape, jnp.float32)
    if shards:
        values = values * levels(rng, shape, shards, -0.22, 0.18)
    return jnp.clip(spiked(values, jax.random.fold_in(rng, 3), *heavy), -limit, limit).astype(kind)


def setup_inputs(seed: int = 0) -> dict:
    key_list = jax.random.split(jax.random.key(seed), 12)
    return {
        "inputs": draw_inputs(jax.random.fold_in(key_list[11], 71), 0),
        "w_query": draw_w_query(jax.random.fold_in(key_list[11], 71), 0),
        "w_key": draw_w_key(jax.random.fold_in(key_list[11], 71), 0),
        "w_value": scatter_about(key_list[3], (D, D), D ** -0.5, 0.125, ((0, 8), (1, 4))),
        "w_out": scatter_about(key_list[4], (D, D), (max(D // 128, 1)) ** -0.5, 1.5, ((0, 4), (1, 8))),
        "gain_one": jnp.clip(1.0 + 0.1 * jax.random.normal(key_list[5], (D,), jnp.float32), 0.5, 1.5).astype(jnp.bfloat16),
        "w_gate": scatter_about(key_list[6], (D, FF), D ** -0.5, 0.125, ((0, 8), (1, 4))),
        "w_up": scatter_about(key_list[7], (D, FF), D ** -0.5, 0.125, ((0, 8), (1, 4))),
        "w_down": scatter_about(key_list[8], (FF, D), FF ** -0.5, 0.0625, ((0, 4), (1, 8))),
        "gain_two": jnp.clip(1.0 + 0.1 * jax.random.normal(key_list[9], (D,), jnp.float32), 0.5, 1.5).astype(jnp.bfloat16),
        "cotangent": heavy_noise(key_list[10], (TOKENS, D), 1.0, 6.0, ((0, 32),), (0, 1, 32, 2.75)),
    }


@jax.custom_vjp
def low(v):
    return lax.optimization_barrier(v.astype(jnp.bfloat16)).astype(jnp.float32)

@jax.custom_vjp
def low_back(v):
    return v

def low_keep(v):
    return (low(v), None)

def low_pass(kept, grad):
    return (grad,)

def back_keep(v):
    return (v, None)

def back_low(kept, grad):
    return (low(grad),)
low.defvjp(low_keep, low_pass)
low_back.defvjp(back_keep, back_low)
epsilon = 1e-05
rope_base = 130000.0

def matmul(left, right):
    return jnp.dot(left, right, precision=lax.Precision.HIGHEST, preferred_element_type=jnp.float32)

def rms_scale(matrix, gain):
    inverse = lax.rsqrt(lax.optimization_barrier(jnp.mean(matrix * matrix, axis=-1, keepdims=True)) + epsilon)
    return matrix * inverse * gain

def rotate(tensor, positions, direction):
    half_size = tensor.shape[-1] // 2
    exponents = jnp.arange(half_size, dtype=jnp.float32) * (-2.0 / tensor.shape[-1])
    frequency = jnp.power(jnp.float32(rope_base), exponents)
    angles = positions.astype(jnp.float32)[:, None] * frequency[None, :]
    cosine = jnp.cos(angles)[:, None, :]
    sines = direction * jnp.sin(angles)[:, None, :]
    former = tensor[..., :half_size]
    latter = tensor[..., half_size:]
    return jnp.concatenate([former * cosine - latter * sines, latter * cosine + former * sines], axis=-1)

def attend(triple):
    queries, key_rows, value_rows = triple
    scaling = HD ** (-0.5)
    scores = low_back(jnp.einsum('qhd,khd->hqk', queries, key_rows, precision=lax.Precision.HIGHEST) * scaling)
    causal = jnp.arange(LEN)[:, None] >= jnp.arange(LEN)[None, :]
    scores = jnp.where(causal[None], scores, -1e+30)
    probabilities = jax.nn.softmax(scores, axis=-1)
    return jnp.einsum('hqk,khd->qhd', low(probabilities), value_rows, precision=lax.Precision.HIGHEST)

def layer(features, w_query, w_key, w_value, w_out, gain_one, w_gate, w_up, w_down, gain_two):
    sequences = features.shape[0] // LEN
    positions = jnp.tile(jnp.arange(LEN), sequences)
    normed_one = low(rms_scale(features, gain_one))
    queries = low(rotate(low_back(matmul(normed_one, w_query)).reshape(-1, H, HD), positions, 1.0))
    key_rows = low(rotate(low_back(matmul(normed_one, w_key)).reshape(-1, H, HD), positions, 1.0))
    value_rows = low_back(low(matmul(normed_one, w_value))).reshape(-1, H, HD)
    shaped = (sequences, LEN, H, HD)
    attended = lax.map(jax.checkpoint(attend), (queries.reshape(shaped), key_rows.reshape(shaped), value_rows.reshape(shaped)))
    attended = low_back(low(attended.reshape(-1, D)))
    hidden_state = features + low_back(matmul(attended, w_out))
    normed_two = low(rms_scale(hidden_state, gain_two))
    gate_proj = low_back(matmul(normed_two, w_gate))
    up_proj = low_back(matmul(normed_two, w_up))
    inner = low(jax.nn.silu(gate_proj) * up_proj)
    return hidden_state + low_back(matmul(inner, w_down))

def reference(inputs, w_query, w_key, w_value, w_out, gain_one, w_gate, w_up, w_down, gain_two, cotangent):
    params = tuple((array.astype(jnp.float32) for array in (w_query, w_key, w_value, w_out, gain_one, w_gate, w_up, w_down, gain_two)))
    features = inputs.astype(jnp.float32).reshape(N_DP, SEQ_DP * LEN, D)
    upstream = cotangent.astype(jnp.float32).reshape(N_DP, SEQ_DP * LEN, D)

    def advance(totals, element):
        segment, segment_grad = element
        result, pull = jax.vjp(layer, segment, *params)
        grads = pull(segment_grad)
        return (jax.tree.map(jnp.add, totals, tuple(grads[1:])), (result.astype(jnp.bfloat16), grads[0]))
    zeros = tuple((jnp.zeros(array.shape, jnp.float32) for array in params))
    totals, (outputs, input_grads) = lax.scan(advance, zeros, (features, upstream))
    return (outputs.reshape(TOKENS, D), input_grads.reshape(TOKENS, D), totals[0], totals[1], totals[2], totals[3], totals[4], totals[5], totals[6], totals[7], totals[8])
```

```python
import jax
import jax.numpy as jnp
from jax import lax
from jax.experimental import pallas as pl
from jax.experimental.pallas import tpu as pltpu
from jax.sharding import PartitionSpec as P

HD = 64
LEN = 1024
LANES = 128
Q_ROWS = 256
HID_TILE = 256
VMEM_BYTES = 60 * 1024 * 1024

epsilon = 1e-05
rope_base = 130000.0

f32 = jnp.float32
bf16 = jnp.bfloat16


def rms_scale(matrix, gain):
    inverse = lax.rsqrt(jnp.mean(matrix * matrix, axis=-1, keepdims=True) + epsilon)
    return matrix * inverse * gain


def norm_back(matrix, gain, upstream):
    result, pull = jax.vjp(rms_scale, matrix, gain)
    return pull(upstream)


def contract(left, right, left_dim, right_dim):
    return lax.dot_general(
        left, right, (((left_dim,), (right_dim,)), ((), ())), preferred_element_type=f32
    )


def rope_tables():
    half = HD // 2
    exponents = jnp.arange(half, dtype=f32) * (-2.0 / HD)
    frequency = jnp.power(f32(rope_base), exponents)
    angles = jnp.arange(LEN).astype(f32)[:, None] * frequency[None, :]
    cosine, sine = jnp.cos(angles), jnp.sin(angles)
    reps = LANES // HD
    return (
        jnp.concatenate([cosine, cosine] * reps, axis=1),
        jnp.concatenate([-sine, sine] * reps, axis=1),
    )


def turn(values, cosine, sine):
    lane = lax.broadcasted_iota(jnp.int32, values.shape, 1)
    other = jnp.where(
        lane % HD < HD // 2,
        pltpu.roll(values, LANES - HD // 2, 1),
        pltpu.roll(values, HD // 2, 1),
    )
    return values * cosine + other * sine


def project_kernel(x_ref, w_ref, cos_ref, sin_ref, out_ref):
    product = jnp.dot(x_ref[...], w_ref[...], preferred_element_type=f32)
    cosine, sine = cos_ref[...], sin_ref[...]
    out_ref[:, :LANES] = turn(product[:, :LANES], cosine, sine).astype(bf16)
    out_ref[:, LANES : 2 * LANES] = turn(product[:, LANES : 2 * LANES], cosine, sine).astype(bf16)
    out_ref[:, 2 * LANES :] = product[:, 2 * LANES :].astype(bf16)


def project(tokens, weights, columns, cosine, sine):
    rows, width = tokens.shape
    tile = 3 * LANES
    tile_rows = 512
    return pl.pallas_call(
        project_kernel,
        grid=(rows // tile_rows, columns // tile),
        in_specs=[
            pl.BlockSpec((tile_rows, width), lambda m, n: (m, 0)),
            pl.BlockSpec((width, tile), lambda m, n: (0, n)),
            pl.BlockSpec((tile_rows, LANES), lambda m, n: (m, 0)),
            pl.BlockSpec((tile_rows, LANES), lambda m, n: (m, 0)),
        ],
        out_specs=pl.BlockSpec((tile_rows, tile), lambda m, n: (m, n)),
        out_shape=jax.ShapeDtypeStruct((rows, columns), bf16),
        compiler_params=pltpu.CompilerParams(vmem_limit_bytes=VMEM_BYTES),
        cost_estimate=pl.CostEstimate(
            flops=2 * rows * width * columns,
            bytes_accessed=2 * (rows * width + width * columns + rows * columns),
            transcendentals=0,
        ),
        name="project",
    )(tokens, weights, cosine, sine)


def head_mask(shape, head):
    lane = lax.broadcasted_iota(jnp.int32, shape, 1)
    return lane // HD == head


def attend_kernel(qkv_ref, out_ref):
    length = qkv_ref.shape[0]
    scale = HD ** (-0.5)
    for block in range(length // Q_ROWS):
        low, high = block * Q_ROWS, (block + 1) * Q_ROWS
        total = jnp.zeros((Q_ROWS, LANES), f32)
        row = low + lax.broadcasted_iota(jnp.int32, (Q_ROWS, high), 0)
        col = lax.broadcasted_iota(jnp.int32, (Q_ROWS, high), 1)
        for head in range(LANES // HD):
            query = qkv_ref[low:high, :LANES]
            query = jnp.where(head_mask(query.shape, head), query, 0).astype(bf16)
            value = qkv_ref[:high, 2 * LANES :]
            value = jnp.where(head_mask(value.shape, head), value, 0).astype(bf16)
            scores = contract(query, qkv_ref[:high, LANES : 2 * LANES], 1, 1) * scale
            scores = jnp.where(row >= col, scores, -1e30)
            peak = jnp.max(scores, axis=1, keepdims=True)
            exponent = jnp.exp(scores - peak)
            inverse = 1.0 / jnp.sum(exponent, axis=1, keepdims=True)
            weights = (exponent * inverse).astype(bf16)
            total = total + jnp.dot(weights, value, preferred_element_type=f32)
        out_ref[low:high, :] = total.astype(bf16)


def attend(qkv):
    rows, columns = qkv.shape
    pairs = columns // (3 * LANES)
    return pl.pallas_call(
        attend_kernel,
        grid=(pairs,),
        in_specs=[pl.BlockSpec((rows, 3 * LANES), lambda p: (0, p))],
        out_specs=pl.BlockSpec((rows, LANES), lambda p: (0, p)),
        out_shape=jax.ShapeDtypeStruct((rows, pairs * LANES), bf16),
        compiler_params=pltpu.CompilerParams(vmem_limit_bytes=VMEM_BYTES),
        cost_estimate=pl.CostEstimate(
            flops=8 * rows * rows * pairs * LANES,
            bytes_accessed=8 * rows * pairs * LANES,
            transcendentals=2 * rows * rows * pairs,
        ),
        name="attend",
    )(qkv)


def attend_back_kernel(qkv_ref, grad_ref, cos_ref, sin_ref, out_ref, key_acc, value_acc):
    length = qkv_ref.shape[0]
    scale = HD ** (-0.5)
    key_acc[...] = jnp.zeros_like(key_acc)
    value_acc[...] = jnp.zeros_like(value_acc)
    for block in range(length // Q_ROWS):
        low, high = block * Q_ROWS, (block + 1) * Q_ROWS
        query_total = jnp.zeros((Q_ROWS, LANES), f32)
        key_row = lax.broadcasted_iota(jnp.int32, (high, Q_ROWS), 0)
        query_col = low + lax.broadcasted_iota(jnp.int32, (high, Q_ROWS), 1)
        for head in range(LANES // HD):
            query = qkv_ref[low:high, :LANES]
            query = jnp.where(head_mask(query.shape, head), query, 0).astype(bf16)
            grad = grad_ref[low:high, :]
            grad = jnp.where(head_mask(grad.shape, head), grad, 0).astype(bf16)
            keys = qkv_ref[:high, LANES : 2 * LANES]
            keys_own = jnp.where(head_mask(keys.shape, head), keys, 0).astype(bf16)
            scores = contract(keys, query, 1, 1) * scale
            scores = jnp.where(query_col >= key_row, scores, -1e30)
            peak = jnp.max(scores, axis=0, keepdims=True)
            exponent = jnp.exp(scores - peak)
            inverse = 1.0 / jnp.sum(exponent, axis=0, keepdims=True)
            weights = exponent * inverse
            grad_weights = contract(qkv_ref[:high, 2 * LANES :], grad, 1, 1)
            row_dot = jnp.sum(weights * grad_weights, axis=0, keepdims=True)
            grad_scores = (weights * (grad_weights - row_dot)).astype(bf16)
            value_acc[:high, :] += jnp.dot(weights.astype(bf16), grad, preferred_element_type=f32)
            key_acc[:high, :] += jnp.dot(grad_scores, query, preferred_element_type=f32)
            query_total = query_total + contract(grad_scores, keys_own, 0, 0)
        cosine, sine = cos_ref[low:high, :], sin_ref[low:high, :]
        out_ref[low:high, :LANES] = turn(query_total * scale, cosine, -sine).astype(bf16)
    out_ref[:, LANES : 2 * LANES] = turn(
        key_acc[...] * scale, cos_ref[...], -sin_ref[...]
    ).astype(bf16)
    out_ref[:, 2 * LANES :] = value_acc[...].astype(bf16)


def attend_back(qkv, grad_attended, cosine, sine):
    rows, columns = qkv.shape
    pairs = columns // (3 * LANES)
    return pl.pallas_call(
        attend_back_kernel,
        grid=(pairs,),
        in_specs=[
            pl.BlockSpec((rows, 3 * LANES), lambda p: (0, p)),
            pl.BlockSpec((rows, LANES), lambda p: (0, p)),
            pl.BlockSpec((rows, LANES), lambda p: (0, 0)),
            pl.BlockSpec((rows, LANES), lambda p: (0, 0)),
        ],
        out_specs=pl.BlockSpec((rows, 3 * LANES), lambda p: (0, p)),
        out_shape=jax.ShapeDtypeStruct((rows, columns), bf16),
        scratch_shapes=[pltpu.VMEM((rows, LANES), f32), pltpu.VMEM((rows, LANES), f32)],
        compiler_params=pltpu.CompilerParams(vmem_limit_bytes=VMEM_BYTES),
        cost_estimate=pl.CostEstimate(
            flops=20 * rows * rows * pairs * LANES,
            bytes_accessed=14 * rows * pairs * LANES,
            transcendentals=2 * rows * rows * pairs,
        ),
        name="attend_back",
    )(qkv, grad_attended, cosine, sine)


def feed_kernel(n_ref, c_ref, w_ref, *rest):
    outs = rest[-8:]
    n_out, c_out, inner_out, grad_out, ffn_out, back_out, ffn_acc, back_acc = outs
    step = pl.program_id(0)
    width = inner_out.shape[1]
    piece = n_out.shape[1]
    normed, cot = n_ref[...], c_ref[...]
    both = jnp.dot(normed, w_ref[:, : 2 * width], preferred_element_type=f32)
    gate, up = both[:, :width], both[:, width:]
    d_inner = jnp.dot(cot, w_ref[:, 2 * width :], preferred_element_type=f32)
    sigmoid = jax.nn.sigmoid(gate)
    silu = gate * sigmoid
    inner = (silu * up).astype(bf16)
    d_gate = (d_inner * up * sigmoid * (1.0 + gate * (1.0 - sigmoid))).astype(bf16)
    d_up = (d_inner * silu).astype(bf16)
    inner_out[...] = inner
    grad_out[:, :width] = d_gate
    grad_out[:, width:] = d_up
    start = pl.multiple_of(step * piece, piece)
    n_out[...] = n_ref[:, pl.ds(start, piece)]
    c_out[...] = c_ref[:, pl.ds(start, piece)]
    ffn = contract(inner, w_ref[:, 2 * width :], 1, 1)
    back = contract(grad_out[...], w_ref[:, : 2 * width], 1, 1)

    @pl.when(step == 0)
    def _():
        ffn_acc[...] = ffn
        back_acc[...] = back

    @pl.when(step > 0)
    def _():
        ffn_acc[...] += ffn
        back_acc[...] += back

    @pl.when(step == pl.num_programs(0) - 1)
    def _():
        ffn_out[...] = ffn_acc[...].astype(bf16)
        back_out[...] = back_acc[...].astype(bf16)


def feed(normed, cot, weights, slot, slots, kept):
    rows, width = normed.shape
    hidden = weights.shape[1] // 3
    steps = hidden // HID_TILE
    piece = width // steps
    in_specs = [
        pl.BlockSpec((rows, width), lambda n: (0, 0)),
        pl.BlockSpec((rows, width), lambda n: (0, 0)),
        pl.BlockSpec((width, 3 * HID_TILE), lambda n: (0, n)),
    ]
    args = [normed, cot, weights]
    aliases = {}
    if kept is not None:
        for index, array in enumerate(kept):
            aliases[len(args)] = index
            args.append(array)
            in_specs.append(pl.BlockSpec(memory_space=pl.ANY))
    total = rows * slots
    outs = pl.pallas_call(
        feed_kernel,
        grid=(steps,),
        in_specs=in_specs,
        out_specs=[
            pl.BlockSpec((rows, piece), lambda n: (slot, n)),
            pl.BlockSpec((rows, piece), lambda n: (slot, n)),
            pl.BlockSpec((rows, HID_TILE), lambda n: (slot, n)),
            pl.BlockSpec((rows, 2 * HID_TILE), lambda n: (slot, n)),
            pl.BlockSpec((rows, width), lambda n: (0, 0)),
            pl.BlockSpec((rows, width), lambda n: (0, 0)),
        ],
        out_shape=[
            jax.ShapeDtypeStruct((total, width), bf16),
            jax.ShapeDtypeStruct((total, width), bf16),
            jax.ShapeDtypeStruct((total, hidden), bf16),
            jax.ShapeDtypeStruct((total, 2 * hidden), bf16),
            jax.ShapeDtypeStruct((rows, width), bf16),
            jax.ShapeDtypeStruct((rows, width), bf16),
        ],
        scratch_shapes=[pltpu.VMEM((rows, width), f32), pltpu.VMEM((rows, width), f32)],
        input_output_aliases=aliases,
        compiler_params=pltpu.CompilerParams(vmem_limit_bytes=VMEM_BYTES),
        cost_estimate=pl.CostEstimate(
            flops=12 * rows * width * hidden,
            bytes_accessed=2 * (3 * width * hidden + 8 * rows * width + 3 * rows * hidden),
            transcendentals=rows * hidden,
        ),
        name="feed",
    )(*args)
    return tuple(outs[:4]), outs[4], outs[5]


def interleave(arrays, tile):
    pieces = []
    for start in range(0, arrays[0].shape[1], tile):
        pieces += [array[:, start : start + tile] for array in arrays]
    return jnp.concatenate(pieces, axis=1)


def take_apart(array, tile, count):
    pieces = [array[:, start : start + tile] for start in range(0, array.shape[1], tile)]
    return [jnp.concatenate(pieces[index::count], axis=1) for index in range(count)]


def make_layer(n_dp, n_t):
    def halve(vector):
        for axis, size in (("dp", n_dp), ("tensor", n_t)):
            index = lax.axis_index(axis)
            bit = size // 2
            while bit:
                parts = vector.reshape(2, -1)
                own = (index // bit) % 2
                keep = lax.dynamic_index_in_dim(parts, own, 0, keepdims=False)
                send = lax.dynamic_index_in_dim(parts, 1 - own, 0, keepdims=False)
                vector = keep + lax.ppermute(send, axis, [(i, i ^ bit) for i in range(size)])
                bit //= 2
        return vector

    def on_device(
        inputs, w_query, w_key, w_value, w_out, gain_one, w_gate, w_up, w_down, gain_two, cotangent
    ):
        rows = inputs.shape[0]
        group = LEN // rows
        sequences = n_t // group
        block_cols = w_query.shape[1]
        t = lax.axis_index("tensor")
        g = t % group
        group_ring = [(i, i - i % group + (i % group + 1) % group) for i in range(n_t)]
        ring = [(i, (i + 1) % n_t) for i in range(n_t)]

        def shift(array, amount):
            return lax.ppermute(array, "tensor", [(i, (i + amount) % n_t) for i in range(n_t)])

        def gather_group(own):
            whole = jnp.zeros((group * rows, own.shape[1]), own.dtype)
            block = own
            for step in range(group):
                if step:
                    block = lax.ppermute(block, "tensor", group_ring)
                place = ((g - step) % group) * rows
                whole = lax.dynamic_update_slice(whole, block, (place, 0))
            return whole

        def scatter_group(partial):
            carried = None
            for step in range(group - 1):
                part = partial((g - 1 - step) % group)
                if carried is not None:
                    part = part + carried.astype(f32)
                carried = lax.ppermute(part.astype(bf16), "tensor", group_ring)
            own = partial(g)
            return own if carried is None else own + carried.astype(f32)

        qkv_shard = interleave([w_query, w_key, w_value], LANES)
        att_shard = jnp.concatenate([qkv_shard, w_out.T], axis=1)
        att_full = [
            lax.all_gather(
                att_shard if not j else shift(att_shard, -group * j), "dp", axis=0, tiled=True
            )
            for j in range(sequences)
        ]
        feed_full = lax.all_gather(
            interleave([w_gate, w_up, w_down.T], HID_TILE), "dp", axis=0, tiled=True
        )
        gains = lax.all_gather(jnp.stack([gain_one, gain_two]), "dp", axis=1, tiled=True)
        gain_one_f, gain_two_f = gains[0].astype(f32), gains[1].astype(f32)

        features = inputs.astype(f32)
        normed_one = gather_group(rms_scale(features, gain_one_f).astype(bf16))
        cosine, sine = rope_tables()
        qkv = [project(normed_one, full, 3 * block_cols, cosine, sine) for full in att_full]
        attended = [attend(block) for block in qkv]
        out_t = [full[:, 3 * block_cols :] for full in att_full]
        qkv_w = [full[:, : 3 * block_cols] for full in att_full]

        def mix(block):
            total = None
            for att, weight in zip(attended, out_t):
                part = contract(lax.dynamic_slice_in_dim(att, block * rows, rows, 0), weight, 1, 1)
                total = part if total is None else total + part
            return total

        hidden_state = features + scatter_group(mix)

        normed = rms_scale(hidden_state, gain_two_f).astype(bf16)
        cot = cotangent
        kept = None
        ffn_parts, back_parts = [], []
        for step in range(n_t):
            if step:
                normed = lax.ppermute(normed, "tensor", ring)
                cot = lax.ppermute(cot, "tensor", ring)
            kept, ffn, back = feed(normed, cot, feed_full, step, n_t, kept)
            ffn_parts.append(ffn)
            back_parts.append(back)

        def scatter_ring(parts):
            carried = None
            for part in parts[1:]:
                part = part.astype(f32)
                if carried is not None:
                    part = part + carried.astype(f32)
                carried = lax.ppermute(part.astype(bf16), "tensor", ring)
            own = parts[0].astype(f32)
            return own if carried is None else own + carried.astype(f32)

        d_normed_two = scatter_ring(back_parts)
        output = (hidden_state + scatter_ring(ffn_parts)).astype(bf16)
        n_all, c_all, inner_all, grad_all = kept
        grad_gate_up = lax.psum_scatter(
            contract(n_all, grad_all, 0, 0).astype(bf16), "dp", scatter_dimension=0, tiled=True
        )
        grad_down_t = lax.psum_scatter(
            contract(c_all, inner_all, 0, 0).astype(bf16), "dp", scatter_dimension=0, tiled=True
        )

        hidden_grad, gain_two_part = norm_back(hidden_state, gain_two_f, d_normed_two)
        d_hidden = cotangent.astype(f32) + hidden_grad

        d_mixed = gather_group(d_hidden.astype(bf16))
        d_qkv, grad_qkv = [None] * sequences, [None] * sequences
        grad_out_t = lax.psum_scatter(
            jnp.concatenate([contract(d_mixed, att, 0, 0).astype(bf16) for att in attended], axis=1),
            "dp",
            scatter_dimension=0,
            tiled=True,
        )
        for j in reversed(range(sequences)):
            d_attended = jnp.dot(d_mixed, out_t[j], preferred_element_type=f32).astype(bf16)
            d_qkv[j] = attend_back(qkv[j], d_attended, cosine, sine)
            grad_qkv[j] = lax.psum_scatter(
                contract(normed_one, d_qkv[j], 0, 0).astype(bf16),
                "dp",
                scatter_dimension=0,
                tiled=True,
            )

        def mix_back(block):
            total = None
            for grad, weight in zip(d_qkv, qkv_w):
                part = contract(lax.dynamic_slice_in_dim(grad, block * rows, rows, 0), weight, 1, 1)
                total = part if total is None else total + part
            return total

        d_normed_one = scatter_group(mix_back)
        feature_grad, gain_one_part = norm_back(features, gain_one_f, d_normed_one)
        input_grad = d_hidden + feature_grad

        qkv_sum = grad_qkv[0].astype(f32)
        out_sum = grad_out_t[:, :block_cols].astype(f32)
        for j in range(1, sequences):
            qkv_sum = qkv_sum + shift(grad_qkv[j], group * j).astype(f32)
            piece = grad_out_t[:, j * block_cols : (j + 1) * block_cols]
            out_sum = out_sum + shift(piece, group * j).astype(f32)
        grad_query, grad_key, grad_value = take_apart(qkv_sum, LANES, 3)
        grad_gate, grad_up = take_apart(grad_gate_up.astype(f32), HID_TILE, 2)
        return (
            output,
            input_grad,
            grad_query,
            grad_key,
            grad_value,
            out_sum.T,
            halve(gain_one_part),
            grad_gate,
            grad_up,
            grad_down_t.astype(f32).T,
            halve(gain_two_part),
        )

    return on_device


def solution(mesh):
    return jax.shard_map(
        make_layer(mesh.shape["dp"], mesh.shape["tensor"]),
        mesh=mesh,
        in_specs=(
            P(("dp", "tensor"), None),
            P("dp", "tensor"),
            P("dp", "tensor"),
            P("dp", "tensor"),
            P("tensor", "dp"),
            P("dp"),
            P("dp", "tensor"),
            P("dp", "tensor"),
            P("tensor", "dp"),
            P("dp"),
            P(("dp", "tensor"), None),
        ),
        out_specs=(
            P(("dp", "tensor"), None),
            P(("dp", "tensor"), None),
            P("dp", "tensor"),
            P("dp", "tensor"),
            P("dp", "tensor"),
            P("tensor", "dp"),
            P(("dp", "tensor")),
            P("dp", "tensor"),
            P("dp", "tensor"),
            P("tensor", "dp"),
            P(("dp", "tensor")),
        ),
        check_vma=False,
    )
```
